1024 devices in a mesh: section: 8 (over x, core), expert: 32 (over z, y_lo), dp: 4 (over y_hi).
Axes of the slice: x: 4, y: 8 (y_hi: 4, y_lo: 2; y = y_hi * 2 + y_lo), z: 16, core: 2. Of those that a mesh axis runs over, the one named last changes fastest.
Arguments:
- panel: bfloat16 [12288, 4096], P(('section', 'expert', 'dp')), may hold values from -6 to 6
- norm_gain: float32 [4096], replicated, may hold values from 0.5 to 1.5
- expert_ids: int32 [12288, 8], P(('section', 'expert', 'dp')), may hold values from 0 to 63, all different within a row; in each aligned block of 12 rows (0 to 11, 12 to 23, ...) at most 2 rows name the same one
- gate_scores: float32 [12288, 8], P(('section', 'expert', 'dp')), may hold values from 0.05 to 1
- w_gate: bfloat16 [64, 4096, 768], P('expert', 'dp'), may hold values from -0.09375 to 0.09375
- w_up: bfloat16 [64, 4096, 768], P('expert', 'dp'), may hold values from -0.09375 to 0.09375
- w_down: bfloat16 [64, 768, 4096], P('expert', None, 'dp'), may hold values from -0.21875 to 0.21875
Outputs:
- mixed_out: bfloat16 [12288, 4096], P(('section', 'expert', 'dp'))
The draws below stay inside these ranges and needn't reach their ends.
Inputs may be any that keep to these rules, and one draw needn't show every extreme that they name: `expert_ids`: each row names 8 different experts. In each aligned block of 12 rows (the rows of one device) no expert is named by more than 2 rows, a bound that some block reaches.
All inputs are finite; a program needn't handle non-finite values.
Results may differ from the reference program's by a relative error of at most 0.008.
Values may be sent and summed in bfloat16 or wider, within the bound.
A program may use at most 64 MiB of HBM per device.

```python
import math
import jax
import jax.numpy as jnp
import numpy as np
from jax import lax

D = 4096
FF = 768
EXPERTS = 64
TOP = 8
CAP = 2
TOK_DEV = 12
TOKENS = 12288
N_SECTION = 8
N_EXPERT = 32
N_DP = 4


def levels(key, shape, pieces, low, high):
    def one(position, blocks):
        steps = jax.random.uniform(jax.random.fold_in(jax.random.fold_in(key, 6), position), (blocks,), jnp.float32, low / len(pieces), high / len(pieces))
        return jnp.repeat(jnp.exp(steps), shape[position] // blocks).reshape((-1,) + (1,) * (len(shape) - position - 1))

    loudness = one(*pieces[0])
    for cut in pieces[1:]:
        loudness = loudness * one(*cut)
    return loudness


def deal_out(key, own, number, rows, number_of, top, most, lean):
    sequence = jax.random.permutation(key, number_of)
    crowded, common = load_shares(number_of, rows * top, most, lean, True), load_shares(number_of, rows * top, most, lean, False)
    places = jnp.arange(number_of)

    def named(tallies, rotation):
        used = int((tallies > 0).sum())
        fixed = max(1, used // 4)
        moved = fixed + (places - fixed + rotation * (used - fixed)) % max(1, number_of - fixed)
        return jnp.zeros((number_of,), jnp.int32).at[sequence[jnp.where(places < fixed, places, moved)]].set(jnp.asarray(tallies, jnp.int32))

    tallies = jnp.where(number % 4 == 0, named(crowded, number // 4), named(common, number - number // 4 - 1))
    mixed = jax.random.permutation(jax.random.fold_in(own, 3), number_of)
    source_of, sink = mixed[0:number_of // 2 * 2:2], mixed[1:number_of // 2 * 2:2]
    margin = jnp.minimum(tallies[source_of] - 1, most - tallies[sink]) // 2
    margin = jnp.where((source_of == sequence[0]) | (sink == sequence[0]) | (tallies[sink] == 0), 0, jnp.maximum(margin, 0))
    moved = jax.random.randint(jax.random.fold_in(own, 4), (number_of // 2,), 0, 1 << 20) % (margin + 1)
    tallies = tallies.at[source_of].add(-moved).at[sink].add(moved)
    items = jnp.searchsorted(jnp.cumsum(tallies), jnp.arange(rows * top), side="right").astype(jnp.int32)
    grid = items.reshape(top, rows).T
    grid = grid[jax.random.permutation(jax.random.fold_in(own, 1), rows)]
    rotation = jax.random.randint(jax.random.fold_in(own, 2), (rows, 1), 0, top)
    return jnp.take_along_axis(grid, (jnp.arange(top)[None, :] + rotation) % top, axis=1)


def load_shares(amount, total, bound, slope, full):
    weights = [(1 << 20) // math.isqrt(standing ** slope) + 1 for standing in range(1, amount + 1)]
    largest = bound if full else min(bound, max(-(-total // amount), total * weights[0] // sum(weights)))
    least = 1 if total - largest >= amount - 1 else 0
    given, spare = [largest] + [least] * (amount - 1), total - largest - least * (amount - 1)
    while spare > 0:
        candidates = [i for i in range(1, amount) if given[i] < largest] or [i for i in range(1, amount) if given[i] < bound]
        mass, left = sum([weights[i] for i in candidates]), spare
        for i in candidates:
            addition = min(bound - given[i], max(1, left * weights[i] // mass), spare)
            given[i] = given[i] + addition
            spare = spare - addition
    return np.array(given)


def normal_values(rng, shape, scale, reach, cuts=(), kind=jnp.bfloat16):
    entries = jax.random.normal(rng, shape, jnp.float32) * scale
    if len(cuts) > 0:
        entries = levels(rng, shape, cuts, -0.22, 0.18) * entries
    return jnp.clip(entries, min=-reach, max=reach).astype(kind)


def setup_inputs(seed: int = 0) -> dict:
    splits = jax.random.split(jax.random.key(seed), 8)
    panel = normal_values(splits[0], (TOKENS, D), 1.0, 6.0, ((0, 1024),))
    norm_gain = jnp.clip(1.0 + 0.1 * jax.random.normal(splits[1], (D,), jnp.float32), 0.5, 1.5)
    expert_ids_keys = jax.random.split(jax.random.fold_in(splits[2], 1), TOKENS // TOK_DEV)
    expert_ids_turns = jax.random.permutation(jax.random.fold_in(splits[2], 3), TOKENS // TOK_DEV)
    expert_ids = jax.vmap(lambda own, number: deal_out(jax.random.fold_in(splits[2], 2), own, number, TOK_DEV, EXPERTS, TOP, CAP, 2))(expert_ids_keys, expert_ids_turns).reshape((TOKENS, TOP))
    gate_scores = jnp.clip(jnp.exp(math.log(1.0) - 2.9957323 * jax.random.uniform(splits[3], (TOKENS, TOP), jnp.float32) ** levels(splits[3], (TOKENS, TOP), ((0, 1024),), -0.2, 0.2)), 0.05, 1.0)
    w_gate = normal_values(splits[4], (EXPERTS, D, FF), D ** -0.5, 0.09375, ((0, 32), (1, 4)))
    w_up = normal_values(splits[5], (EXPERTS, D, FF), D ** -0.5, 0.09375, ((0, 32), (1, 4)))
    w_down = normal_values(splits[6], (EXPERTS, FF, D), FF ** -0.5, 0.21875, ((0, 32), (2, 4)))
    return dict(panel=panel, norm_gain=norm_gain, expert_ids=expert_ids, gate_scores=gate_scores, w_gate=w_gate, w_up=w_up, w_down=w_down)


def reference(panel, norm_gain, expert_ids, gate_scores, w_gate, w_up, w_down):
    block_rows = TOK_DEV * N_EXPERT * N_DP
    arrived = jnp.roll(panel, block_rows, axis=0)
    arrived_f = arrived.astype(jnp.float32)
    mean_sq = lax.optimization_barrier(jnp.mean(arrived_f * arrived_f, axis=-1, keepdims=True))
    normed = (arrived_f * lax.rsqrt(mean_sq + 1e-06) * norm_gain).astype(jnp.bfloat16)
    combine = (gate_scores / lax.optimization_barrier(jnp.sum(gate_scores, axis=-1, keepdims=True))).astype(jnp.bfloat16)
    flat_weight = combine.reshape(-1).astype(jnp.float32)
    flat_ids = expert_ids.reshape(-1).astype(jnp.int32)
    ordering = jnp.argsort(flat_ids, stable=True).astype(jnp.int32)
    counts = lax.optimization_barrier(jnp.sum((flat_ids[:, None] == jnp.arange(EXPERTS, dtype=jnp.int32)[None, :]).astype(jnp.int32), axis=0)).astype(jnp.int32)
    starts = (jnp.cumsum(counts) - counts).astype(jnp.int32)
    window = N_SECTION * N_EXPERT * N_DP * CAP
    padded = jnp.concatenate([ordering, jnp.zeros((window,), jnp.int32)])
    part_width = D // N_DP

    def expert_pass(total, operands):
        gate_e, up_e, down_e, first_row, count = operands
        picked = lax.dynamic_slice_in_dim(padded, first_row, window)
        live = (jnp.arange(window, dtype=jnp.int32) < count).astype(jnp.float32)
        token_rows = (picked // TOP).astype(jnp.int32)
        inputs = normed[token_rows]
        gate = jnp.zeros((window, FF), jnp.float32)
        up_sum = jnp.zeros((window, FF), jnp.float32)
        for piece_index in range(N_DP):
            offset = piece_index * part_width
            gate_piece = jnp.dot(inputs[:, offset:offset + part_width], gate_e[offset:offset + part_width], preferred_element_type=jnp.float32)
            up_piece = jnp.dot(inputs[:, offset:offset + part_width], up_e[offset:offset + part_width], preferred_element_type=jnp.float32)
            gate_round = lax.optimization_barrier(gate_piece.astype(jnp.bfloat16))
            up_round = lax.optimization_barrier(up_piece.astype(jnp.bfloat16))
            gate = gate + gate_round.astype(jnp.float32)
            up_sum = up_sum + up_round.astype(jnp.float32)
        hidden = (jax.nn.silu(gate) * up_sum).astype(jnp.bfloat16)
        expert_out = jnp.dot(hidden, down_e, preferred_element_type=jnp.float32).astype(jnp.bfloat16)
        weight_rows = flat_weight[picked] * live
        total = total.at[token_rows].add(weight_rows[:, None] * expert_out.astype(jnp.float32))
        return (total, None)
    mixed_total, unused = lax.scan(expert_pass, arrived_f, (w_gate, w_up, w_down, starts, counts))
    return mixed_total.astype(jnp.bfloat16)
```

```python
import jax
import jax.numpy as jnp
from jax import lax
from jax.sharding import PartitionSpec as P

CAP = 2


def passed_along(shard, axis, by):
    peers = lax.axis_size(axis)
    return lax.ppermute(shard, axis, [(i, (i + by) % peers) for i in range(peers)])


def per_device(panel, norm_gain, expert_ids, gate_scores, w_gate, w_up, w_down):
    arrived = passed_along(panel, "section", 1)
    arrived_f = arrived.astype(jnp.float32)
    mean_sq = jnp.mean(arrived_f * arrived_f, axis=-1, keepdims=True)
    normed = (arrived_f * lax.rsqrt(mean_sq + 1e-06) * norm_gain).astype(jnp.bfloat16)
    experts_here = w_gate.shape[0]
    width_part = w_gate.shape[1]
    expert_groups = lax.axis_size("expert")
    dp_groups = lax.axis_size("dp")
    tokens_here = expert_ids.shape[0]
    top_k = expert_ids.shape[1]
    slot_rows = experts_here * CAP
    all_slots = expert_groups * slot_rows
    flat_ids = expert_ids.reshape(-1)
    expert_hits = (
        flat_ids[:, None] == jnp.arange(expert_groups * experts_here, dtype=jnp.int32)[None, :]
    ).astype(jnp.int32)
    earlier = jnp.cumsum(expert_hits, axis=0) - expert_hits
    slot_index = jnp.sum(earlier * expert_hits, axis=1)
    target = flat_ids * CAP + slot_index
    placed = (target[:, None] == jnp.arange(all_slots, dtype=jnp.int32)[None, :]).reshape(
        tokens_here, top_k, all_slots
    )
    occupied = jnp.any(placed, axis=1).astype(jnp.bfloat16).reshape(
        tokens_here, expert_groups, slot_rows
    )
    normed_parts = normed.reshape(tokens_here, dp_groups, width_part)
    send_rows = jnp.einsum(
        "tes,tpw->epsw", occupied, normed_parts, preferred_element_type=jnp.float32
    ).astype(jnp.bfloat16)
    devices = expert_groups * dp_groups
    outgoing = send_rows.reshape(devices, slot_rows, width_part)
    incoming = lax.all_to_all(
        outgoing, ("expert", "dp"), split_axis=0, concat_axis=0, tiled=True
    )
    grouped = incoming.reshape(devices, experts_here, CAP, width_part)
    gate_part = jnp.einsum("nxcd,xdf->nxcf", grouped, w_gate, preferred_element_type=jnp.float32)
    up_part = jnp.einsum("nxcd,xdf->nxcf", grouped, w_up, preferred_element_type=jnp.float32)
    gate_full, up_full = (
        lax.psum(gate_part.astype(jnp.bfloat16), "dp").astype(jnp.float32),
        lax.psum(up_part.astype(jnp.bfloat16), "dp").astype(jnp.float32),
    )
    hidden = (jax.nn.silu(gate_full) * up_full).astype(jnp.bfloat16)
    expert_out = jnp.einsum(
        "nxcf,xfd->nxcd", hidden, w_down, preferred_element_type=jnp.float32
    ).astype(jnp.bfloat16)
    returning = expert_out.reshape(devices, slot_rows, width_part)
    returned = lax.all_to_all(
        returning, ("expert", "dp"), split_axis=0, concat_axis=0, tiled=True
    )
    back = returned.reshape(expert_groups, dp_groups, slot_rows, width_part)
    weights = (gate_scores / jnp.sum(gate_scores, axis=-1, keepdims=True)).astype(jnp.bfloat16)
    combine = jnp.sum(
        jnp.where(placed, weights[:, :, None].astype(jnp.float32), 0.0), axis=1
    ).astype(jnp.bfloat16).reshape(tokens_here, expert_groups, slot_rows)
    mixed = jnp.einsum("tes,epsw->tpw", combine, back, preferred_element_type=jnp.float32)
    mixed_out = arrived_f + mixed.reshape(tokens_here, dp_groups * width_part)
    return mixed_out.astype(jnp.bfloat16)


def solution(mesh):
    in_specs = (
        P(("section", "expert", "dp"), None),
        P(),
        P(("section", "expert", "dp"), None),
        P(("section", "expert", "dp"), None),
        P("expert", "dp", None),
        P("expert", "dp", None),
        P("expert", None, "dp"),
    )
    out_specs = P(("section", "expert", "dp"), None)
    return jax.shard_map(
        per_device, mesh=mesh, in_specs=in_specs, out_specs=out_specs, check_vma=False
    )
```

```python
import jax
import jax.numpy as jnp
from jax import lax
from jax.sharding import PartitionSpec as P

CAP = 2


def passed_along(shard, axis, by):
    peers = lax.axis_size(axis)
    return lax.ppermute(shard, axis, [(i, (i + by) % peers) for i in range(peers)])


def per_device(panel, norm_gain, expert_ids, gate_scores, w_gate, w_up, w_down):
    arrived = passed_along(panel, "section", 1)
    arrived_f = arrived.astype(jnp.float32)
    mean_sq = jnp.mean(arrived_f * arrived_f, axis=-1, keepdims=True)
    normed = (arrived_f * lax.rsqrt(mean_sq + 1e-06) * norm_gain).astype(jnp.bfloat16)
    experts_here = w_gate.shape[0]
    width_part = w_gate.shape[1]
    expert_groups = lax.axis_size("expert")
    dp_groups = lax.axis_size("dp")
    tokens_here = expert_ids.shape[0]
    top_k = expert_ids.shape[1]
    slot_rows = experts_here * CAP
    all_slots = expert_groups * slot_rows
    flat_ids = expert_ids.reshape(-1)
    expert_hits = (
        flat_ids[:, None] == jnp.arange(expert_groups * experts_here, dtype=jnp.int32)[None, :]
    ).astype(jnp.int32)
    earlier = jnp.cumsum(expert_hits, axis=0) - expert_hits
    slot_index = jnp.sum(earlier * expert_hits, axis=1)
    target = flat_ids * CAP + slot_index
    placed = (target[:, None] == jnp.arange(all_slots, dtype=jnp.int32)[None, :]).reshape(
        tokens_here, top_k, all_slots
    )
    occupied = jnp.any(placed, axis=1).astype(jnp.bfloat16).reshape(
        tokens_here, expert_groups, slot_rows
    )
    normed_parts = normed.reshape(tokens_here, dp_groups, width_part)
    send_rows = jnp.einsum(
        "tes,tpw->epsw", occupied, normed_parts, preferred_element_type=jnp.float32
    ).astype(jnp.bfloat16)
    devices = expert_groups * dp_groups
    outgoing = send_rows.reshape(devices, slot_rows, width_part)
    incoming = lax.all_to_all(
        outgoing, ("expert", "dp"), split_axis=0, concat_axis=0, tiled=True
    )
    grouped = incoming.reshape(devices, experts_here, CAP, width_part)
    gate_part = jnp.einsum("nxcd,xdf->nxcf", grouped, w_gate, preferred_element_type=jnp.float32)
    up_part = jnp.einsum("nxcd,xdf->nxcf", grouped, w_up, preferred_element_type=jnp.float32)
    chunks = gate_part.shape[0] // dp_groups
    parts = jnp.stack(
        [
            gate_part.reshape(dp_groups, chunks, experts_here, CAP, -1),
            up_part.reshape(dp_groups, chunks, experts_here, CAP, -1),
        ],
        axis=1,
    ).astype(jnp.bfloat16)
    parts = lax.all_to_all(parts, "dp", split_axis=0, concat_axis=0, tiled=False)
    summed = jnp.sum(parts.astype(jnp.float32), axis=0)
    gate_full, up_full = summed[0], summed[1]
    hidden_chunk = (jax.nn.silu(gate_full) * up_full).astype(jnp.bfloat16)
    hidden = lax.all_gather(hidden_chunk, "dp", axis=0, tiled=True)
    hidden = hidden.reshape(devices, experts_here, CAP, -1)
    expert_out = jnp.einsum(
        "nxcf,xfd->nxcd", hidden, w_down, preferred_element_type=jnp.float32
    ).astype(jnp.bfloat16)
    returning = expert_out.reshape(devices, slot_rows, width_part)
    returned = lax.all_to_all(
        returning, ("expert", "dp"), split_axis=0, concat_axis=0, tiled=True
    )
    back = returned.reshape(expert_groups, dp_groups, slot_rows, width_part)
    weights = (gate_scores / jnp.sum(gate_scores, axis=-1, keepdims=True)).astype(jnp.bfloat16)
    combine = jnp.sum(
        jnp.where(placed, weights[:, :, None].astype(jnp.float32), 0.0), axis=1
    ).astype(jnp.bfloat16).reshape(tokens_here, expert_groups, slot_rows)
    mixed = jnp.einsum("tes,epsw->tpw", combine, back, preferred_element_type=jnp.float32)
    mixed_out = arrived_f + mixed.reshape(tokens_here, dp_groups * width_part)
    return mixed_out.astype(jnp.bfloat16)


def solution(mesh):
    in_specs = (
        P(("section", "expert", "dp"), None),
        P(),
        P(("section", "expert", "dp"), None),
        P(("section", "expert", "dp"), None),
        P("expert", "dp", None),
        P("expert", "dp", None),
        P("expert", None, "dp"),
    )
    out_specs = P(("section", "expert", "dp"), None)
    return jax.shard_map(
        per_device, mesh=mesh, in_specs=in_specs, out_specs=out_specs, check_vma=False
    )
```

```python
import jax
import jax.numpy as jnp
from jax import lax
from jax.sharding import PartitionSpec as P

CAP = 2


def passed_along(shard, axis, by):
    peers = lax.axis_size(axis)
    return lax.ppermute(shard, axis, [(i, (i + by) % peers) for i in range(peers)])


def per_device(panel, norm_gain, expert_ids, gate_scores, w_gate, w_up, w_down):
    arrived = passed_along(panel, "section", 1)
    arrived_f = arrived.astype(jnp.float32)
    mean_sq = jnp.mean(arrived_f * arrived_f, axis=-1, keepdims=True)
    normed = (arrived_f * lax.rsqrt(mean_sq + 1e-06) * norm_gain).astype(jnp.bfloat16)
    experts_here = w_gate.shape[0]
    width_part = w_gate.shape[1]
    expert_groups = lax.axis_size("expert")
    dp_groups = lax.axis_size("dp")
    tokens_here = expert_ids.shape[0]
    top_k = expert_ids.shape[1]
    slot_rows = experts_here * CAP
    all_slots = expert_groups * slot_rows
    flat_ids = expert_ids.reshape(-1)
    expert_hits = (
        flat_ids[:, None] == jnp.arange(expert_groups * experts_here, dtype=jnp.int32)[None, :]
    ).astype(jnp.int32)
    earlier = jnp.cumsum(expert_hits, axis=0) - expert_hits
    slot_index = jnp.sum(earlier * expert_hits, axis=1)
    target = flat_ids * CAP + slot_index
    placed = (target[:, None] == jnp.arange(all_slots, dtype=jnp.int32)[None, :]).reshape(
        tokens_here, top_k, all_slots
    )
    occupied = jnp.any(placed, axis=1).astype(jnp.bfloat16).reshape(
        tokens_here, expert_groups, experts_here, CAP
    )
    weights = (gate_scores / jnp.sum(gate_scores, axis=-1, keepdims=True)).astype(jnp.bfloat16)
    combine = jnp.sum(
        jnp.where(placed, weights[:, :, None].astype(jnp.float32), 0.0), axis=1
    ).astype(jnp.bfloat16).reshape(tokens_here, expert_groups, experts_here, CAP)
    normed_parts = normed.reshape(tokens_here, dp_groups, width_part)
    devices = expert_groups * dp_groups
    chunks = devices // dp_groups
    send_rows = jnp.einsum(
        "texc,tpw->xepcw", occupied, normed_parts, preferred_element_type=jnp.float32
    ).astype(jnp.bfloat16)
    mixed = jnp.zeros((tokens_here, dp_groups, width_part), jnp.float32)
    for x in range(experts_here):
        outgoing = send_rows[x].reshape(devices, CAP, width_part)
        grouped = lax.all_to_all(
            outgoing, ("expert", "dp"), split_axis=0, concat_axis=0, tiled=True
        )
        gate_part = jnp.einsum(
            "ncd,df->ncf", grouped, w_gate[x], preferred_element_type=jnp.float32
        )
        up_part = jnp.einsum("ncd,df->ncf", grouped, w_up[x], preferred_element_type=jnp.float32)
        parts = jnp.stack(
            [
                gate_part.reshape(dp_groups, chunks, CAP, -1),
                up_part.reshape(dp_groups, chunks, CAP, -1),
            ],
            axis=1,
        ).astype(jnp.bfloat16)
        parts = lax.all_to_all(parts, "dp", split_axis=0, concat_axis=0, tiled=False)
        summed = jnp.sum(parts.astype(jnp.float32), axis=0)
        hidden_chunk = (jax.nn.silu(summed[0]) * summed[1]).astype(jnp.bfloat16)
        hidden = lax.all_gather(hidden_chunk, "dp", axis=0, tiled=True)
        expert_out = jnp.einsum(
            "ncf,fd->ncd", hidden, w_down[x], preferred_element_type=jnp.float32
        ).astype(jnp.bfloat16)
        returned = lax.all_to_all(
            expert_out, ("expert", "dp"), split_axis=0, concat_axis=0, tiled=True
        )
        back = returned.reshape(expert_groups, dp_groups, CAP, width_part)
        mixed = mixed + jnp.einsum(
            "tec,epcw->tpw", combine[:, :, x], back, preferred_element_type=jnp.float32
        )
    mixed_out = arrived_f + mixed.reshape(tokens_here, dp_groups * width_part)
    return mixed_out.astype(jnp.bfloat16)


def solution(mesh):
    in_specs = (
        P(("section", "expert", "dp"), None),
        P(),
        P(("section", "expert", "dp"), None),
        P(("section", "expert", "dp"), None),
        P("expert", "dp", None),
        P("expert", "dp", None),
        P("expert", None, "dp"),
    )
    out_specs = P(("section", "expert", "dp"), None)
    return jax.shard_map(
        per_device, mesh=mesh, in_specs=in_specs, out_specs=out_specs, check_vma=False
    )
```

```python
import jax
import jax.numpy as jnp
from jax import lax
from jax.sharding import PartitionSpec as P

CAP = 2


def passed_along(shard, axis, by):
    peers = lax.axis_size(axis)
    return lax.ppermute(shard, axis, [(i, (i + by) % peers) for i in range(peers)])


def per_device(panel, norm_gain, expert_ids, gate_scores, w_gate, w_up, w_down):
    arrived = passed_along(panel, "section", 1)
    arrived_f = arrived.astype(jnp.float32)
    mean_sq = jnp.mean(arrived_f * arrived_f, axis=-1, keepdims=True)
    normed = (arrived_f * lax.rsqrt(mean_sq + 1e-06) * norm_gain).astype(jnp.bfloat16)
    experts_here = w_gate.shape[0]
    width_part = w_gate.shape[1]
    expert_groups = lax.axis_size("expert")
    dp_groups = lax.axis_size("dp")
    tokens_here = expert_ids.shape[0]
    top_k = expert_ids.shape[1]
    slot_rows = experts_here * CAP
    all_slots = expert_groups * slot_rows
    flat_ids = expert_ids.reshape(-1)
    expert_hits = (
        flat_ids[:, None] == jnp.arange(expert_groups * experts_here, dtype=jnp.int32)[None, :]
    ).astype(jnp.int32)
    earlier = jnp.cumsum(expert_hits, axis=0) - expert_hits
    slot_index = jnp.sum(earlier * expert_hits, axis=1)
    target = flat_ids * CAP + slot_index
    placed = (target[:, None] == jnp.arange(all_slots, dtype=jnp.int32)[None, :]).reshape(
        tokens_here, top_k, all_slots
    )
    occupied = jnp.any(placed, axis=1).astype(jnp.bfloat16).reshape(
        tokens_here, expert_groups, slot_rows
    )
    devices = expert_groups * dp_groups
    normed_parts = normed.reshape(tokens_here, dp_groups, width_part)
    gathered = lax.all_to_all(normed_parts, "dp", split_axis=1, concat_axis=0, tiled=True)
    gathered = lax.all_gather(gathered, "expert", axis=0, tiled=True)
    tokens_all = gathered.reshape(devices, tokens_here, width_part)
    ids_all = lax.all_gather(expert_ids, ("expert", "dp"), axis=0, tiled=True)
    ids_all = ids_all.reshape(devices, tokens_here, top_k)
    mine = lax.axis_index("expert") * experts_here + jnp.arange(experts_here, dtype=jnp.int32)
    hits = jnp.any(ids_all[:, :, :, None] == mine[None, None, None, :], axis=2).astype(jnp.int32)
    before = jnp.cumsum(hits, axis=1) - hits
    pick = (hits[:, :, :, None] == 1) & (
        before[:, :, :, None] == jnp.arange(CAP, dtype=jnp.int32)[None, None, None, :]
    )
    grouped = jnp.einsum(
        "ntxc,ntw->nxcw", pick.astype(jnp.bfloat16), tokens_all, preferred_element_type=jnp.float32
    ).astype(jnp.bfloat16)
    gate_part = jnp.einsum("nxcd,xdf->nxcf", grouped, w_gate, preferred_element_type=jnp.float32)
    up_part = jnp.einsum("nxcd,xdf->nxcf", grouped, w_up, preferred_element_type=jnp.float32)
    chunks = gate_part.shape[0] // dp_groups
    parts = jnp.stack(
        [
            gate_part.reshape(dp_groups, chunks, experts_here, CAP, -1),
            up_part.reshape(dp_groups, chunks, experts_here, CAP, -1),
        ],
        axis=1,
    ).astype(jnp.bfloat16)
    parts = lax.all_to_all(parts, "dp", split_axis=0, concat_axis=0, tiled=False)
    summed = jnp.sum(parts.astype(jnp.float32), axis=0)
    gate_full, up_full = summed[0], summed[1]
    hidden_chunk = (jax.nn.silu(gate_full) * up_full).astype(jnp.bfloat16)
    hidden = lax.all_gather(hidden_chunk, "dp", axis=0, tiled=True)
    hidden = hidden.reshape(devices, experts_here, CAP, -1)
    expert_out = jnp.einsum(
        "nxcf,xfd->nxcd", hidden, w_down, preferred_element_type=jnp.float32
    ).astype(jnp.bfloat16)
    returning = expert_out.reshape(devices, slot_rows, width_part)
    returned = lax.all_to_all(
        returning, ("expert", "dp"), split_axis=0, concat_axis=0, tiled=True
    )
    back = returned.reshape(expert_groups, dp_groups, slot_rows, width_part)
    weights = (gate_scores / jnp.sum(gate_scores, axis=-1, keepdims=True)).astype(jnp.bfloat16)
    combine = jnp.sum(
        jnp.where(placed, weights[:, :, None].astype(jnp.float32), 0.0), axis=1
    ).astype(jnp.bfloat16).reshape(tokens_here, expert_groups, slot_rows)
    mixed = jnp.einsum("tes,epsw->tpw", combine, back, preferred_element_type=jnp.float32)
    mixed_out = arrived_f + mixed.reshape(tokens_here, dp_groups * width_part)
    return mixed_out.astype(jnp.bfloat16)


def solution(mesh):
    in_specs = (
        P(("section", "expert", "dp"), None),
        P(),
        P(("section", "expert", "dp"), None),
        P(("section", "expert", "dp"), None),
        P("expert", "dp", None),
        P("expert", "dp", None),
        P("expert", None, "dp"),
    )
    out_specs = P(("section", "expert", "dp"), None)
    return jax.shard_map(
        per_device, mesh=mesh, in_specs=in_specs, out_specs=out_specs, check_vma=False
    )
```

```python
import jax
import jax.numpy as jnp
from jax import lax
from jax.sharding import PartitionSpec as P

CAP = 2


def passed_along(shard, axis, by):
    peers = lax.axis_size(axis)
    return lax.ppermute(shard, axis, [(i, (i + by) % peers) for i in range(peers)])


def per_device(panel, norm_gain, expert_ids, gate_scores, w_gate, w_up, w_down):
    arrived = passed_along(panel, "section", 1)
    arrived_f = arrived.astype(jnp.float32)
    mean_sq = jnp.mean(arrived_f * arrived_f, axis=-1, keepdims=True)
    normed = (arrived_f * lax.rsqrt(mean_sq + 1e-06) * norm_gain).astype(jnp.bfloat16)
    experts_here = w_gate.shape[0]
    width_part = w_gate.shape[1]
    expert_groups = lax.axis_size("expert")
    dp_groups = lax.axis_size("dp")
    tokens_here = expert_ids.shape[0]
    top_k = expert_ids.shape[1]
    slot_rows = experts_here * CAP
    all_slots = expert_groups * slot_rows
    flat_ids = expert_ids.reshape(-1)
    expert_hits = (
        flat_ids[:, None] == jnp.arange(expert_groups * experts_here, dtype=jnp.int32)[None, :]
    ).astype(jnp.int32)
    earlier = jnp.cumsum(expert_hits, axis=0) - expert_hits
    slot_index = jnp.sum(earlier * expert_hits, axis=1)
    target = flat_ids * CAP + slot_index
    placed = (target[:, None] == jnp.arange(all_slots, dtype=jnp.int32)[None, :]).reshape(
        tokens_here, top_k, all_slots
    )
    occupied = jnp.any(placed, axis=1).astype(jnp.bfloat16).reshape(
        tokens_here, expert_groups, slot_rows
    )
    normed_parts = normed.reshape(tokens_here, dp_groups, width_part)
    send_rows = jnp.einsum(
        "tes,tpw->pesw", occupied, normed_parts, preferred_element_type=jnp.float32
    ).astype(jnp.bfloat16)
    devices = expert_groups * dp_groups
    outgoing = send_rows.reshape(devices, slot_rows, width_part)
    incoming = lax.all_to_all(
        outgoing, ("dp", "expert"), split_axis=0, concat_axis=0, tiled=True
    )
    grouped = incoming.reshape(devices, experts_here, CAP, width_part)
    gate_part = jnp.einsum("nxcd,xdf->nxcf", grouped, w_gate, preferred_element_type=jnp.float32)
    up_part = jnp.einsum("nxcd,xdf->nxcf", grouped, w_up, preferred_element_type=jnp.float32)
    chunks = gate_part.shape[0] // dp_groups
    parts = jnp.stack(
        [
            gate_part.reshape(dp_groups, chunks, experts_here, CAP, -1),
            up_part.reshape(dp_groups, chunks, experts_here, CAP, -1),
        ],
        axis=1,
    ).astype(jnp.bfloat16)
    parts = lax.all_to_all(parts, "dp", split_axis=0, concat_axis=0, tiled=False)
    summed = jnp.sum(parts.astype(jnp.float32), axis=0)
    gate_full, up_full = summed[0], summed[1]
    hidden_chunk = (jax.nn.silu(gate_full) * up_full).astype(jnp.bfloat16)
    hidden = lax.all_gather(hidden_chunk, "dp", axis=0, tiled=True)
    hidden = hidden.reshape(devices, experts_here, CAP, -1)
    expert_out = jnp.einsum(
        "nxcf,xfd->nxcd", hidden, w_down, preferred_element_type=jnp.float32
    ).astype(jnp.bfloat16)
    returning = expert_out.reshape(devices, slot_rows, width_part)
    returned = lax.all_to_all(
        returning, ("dp", "expert"), split_axis=0, concat_axis=0, tiled=True
    )
    back = returned.reshape(dp_groups, all_slots, width_part)
    weights = (gate_scores / jnp.sum(gate_scores, axis=-1, keepdims=True)).astype(jnp.bfloat16)
    combine = jnp.sum(
        jnp.where(placed, weights[:, :, None].astype(jnp.float32), 0.0), axis=1
    ).astype(jnp.bfloat16)
    mixed = jnp.einsum("tk,pkw->tpw", combine, back, preferred_element_type=jnp.float32)
    mixed_out = arrived_f + mixed.reshape(tokens_here, dp_groups * width_part)
    return mixed_out.astype(jnp.bfloat16)


def solution(mesh):
    in_specs = (
        P(("section", "expert", "dp"), None),
        P(),
        P(("section", "expert", "dp"), None),
        P(("section", "expert", "dp"), None),
        P("expert", "dp", None),
        P("expert", "dp", None),
        P("expert", None, "dp"),
    )
    out_specs = P(("section", "expert", "dp"), None)
    return jax.shard_map(
        per_device, mesh=mesh, in_specs=in_specs, out_specs=out_specs, check_vma=False
    )
```

```python
import jax
import jax.numpy as jnp
from jax import lax
from jax.sharding import PartitionSpec as P

CAP = 2


def passed_along(shard, axis, by):
    peers = lax.axis_size(axis)
    return lax.ppermute(shard, axis, [(i, (i + by) % peers) for i in range(peers)])


def per_device(panel, norm_gain, expert_ids, gate_scores, w_gate, w_up, w_down):
    arrived = passed_along(panel, "section", 1)
    arrived_f = arrived.astype(jnp.float32)
    mean_sq = jnp.mean(arrived_f * arrived_f, axis=-1, keepdims=True)
    normed = (arrived_f * lax.rsqrt(mean_sq + 1e-06) * norm_gain).astype(jnp.bfloat16)
    experts_here = w_gate.shape[0]
    width_part = w_gate.shape[1]
    expert_groups = lax.axis_size("expert")
    dp_groups = lax.axis_size("dp")
    tokens_here = expert_ids.shape[0]
    top_k = expert_ids.shape[1]
    slot_rows = experts_here * CAP
    all_slots = expert_groups * slot_rows
    flat_ids = expert_ids.reshape(-1)
    expert_hits = (
        flat_ids[:, None] == jnp.arange(expert_groups * experts_here, dtype=jnp.int32)[None, :]
    ).astype(jnp.int32)
    earlier = jnp.cumsum(expert_hits, axis=0) - expert_hits
    slot_index = jnp.sum(earlier * expert_hits, axis=1)
    target = flat_ids * CAP + slot_index
    placed = (target[:, None] == jnp.arange(all_slots, dtype=jnp.int32)[None, :]).reshape(
        tokens_here, top_k, all_slots
    )
    occupied = jnp.any(placed, axis=1).astype(jnp.bfloat16).reshape(
        tokens_here, expert_groups, experts_here, CAP
    )
    weights = (gate_scores / jnp.sum(gate_scores, axis=-1, keepdims=True)).astype(jnp.bfloat16)
    combine = jnp.sum(
        jnp.where(placed, weights[:, :, None].astype(jnp.float32), 0.0), axis=1
    ).astype(jnp.bfloat16).reshape(tokens_here, expert_groups, experts_here, CAP)
    normed_parts = normed.reshape(tokens_here, dp_groups, width_part)
    devices = expert_groups * dp_groups
    chunks = devices // dp_groups
    send_rows = jnp.einsum(
        "texc,tpw->xepcw", occupied, normed_parts, preferred_element_type=jnp.float32
    ).astype(jnp.bfloat16)
    mixed = jnp.zeros((tokens_here, dp_groups, width_part), jnp.float32)
    for x in range(experts_here):
        outgoing = send_rows[x].reshape(devices, CAP, width_part)
        grouped = lax.all_to_all(
            outgoing, ("expert", "dp"), split_axis=0, concat_axis=0, tiled=True
        )
        gate_part = jnp.einsum(
            "ncd,df->ncf", grouped, w_gate[x], preferred_element_type=jnp.float32
        )
        up_part = jnp.einsum("ncd,df->ncf", grouped, w_up[x], preferred_element_type=jnp.float32)
        parts = jnp.stack(
            [
                gate_part.reshape(dp_groups, chunks, CAP, -1),
                up_part.reshape(dp_groups, chunks, CAP, -1),
            ],
            axis=1,
        ).astype(jnp.bfloat16)
        here = lax.axis_index("dp")
        summed = lax.dynamic_index_in_dim(parts, here, 0, keepdims=False).astype(jnp.float32)
        for shift in range(1, dp_groups):
            piece = lax.dynamic_index_in_dim(parts, (here + shift) % dp_groups, 0, keepdims=False)
            summed = summed + passed_along(piece, "dp", shift).astype(jnp.float32)
        hidden_chunk = (jax.nn.silu(summed[0]) * summed[1]).astype(jnp.bfloat16)
        hidden = lax.all_gather(hidden_chunk, "dp", axis=0, tiled=True)
        expert_out = jnp.einsum(
            "ncf,fd->ncd", hidden, w_down[x], preferred_element_type=jnp.float32
        ).astype(jnp.bfloat16)
        returned = lax.all_to_all(
            expert_out, ("expert", "dp"), split_axis=0, concat_axis=0, tiled=True
        )
        back = returned.reshape(expert_groups, dp_groups, CAP, width_part)
        mixed = mixed + jnp.einsum(
            "tec,epcw->tpw", combine[:, :, x], back, preferred_element_type=jnp.float32
        )
    mixed_out = arrived_f + mixed.reshape(tokens_here, dp_groups * width_part)
    return mixed_out.astype(jnp.bfloat16)


def solution(mesh):
    in_specs = (
        P(("section", "expert", "dp"), None),
        P(),
        P(("section", "expert", "dp"), None),
        P(("section", "expert", "dp"), None),
        P("expert", "dp", None),
        P("expert", "dp", None),
        P("expert", None, "dp"),
    )
    out_specs = P(("section", "expert", "dp"), None)
    return jax.shard_map(
        per_device, mesh=mesh, in_specs=in_specs, out_specs=out_specs, check_vma=False
    )
```

```python
import jax
import jax.numpy as jnp
from jax import lax
from jax.sharding import PartitionSpec as P

CAP = 2


def passed_along(shard, axis, by):
    peers = lax.axis_size(axis)
    return lax.ppermute(shard, axis, [(i, (i + by) % peers) for i in range(peers)])


def per_device(panel, norm_gain, expert_ids, gate_scores, w_gate, w_up, w_down):
    arrived = passed_along(panel, "section", 1)
    arrived_f = arrived.astype(jnp.float32)
    mean_sq = jnp.mean(arrived_f * arrived_f, axis=-1, keepdims=True)
    normed = (arrived_f * lax.rsqrt(mean_sq + 1e-06) * norm_gain).astype(jnp.bfloat16)
    experts_here = w_gate.shape[0]
    width_part = w_gate.shape[1]
    expert_groups = lax.axis_size("expert")
    dp_groups = lax.axis_size("dp")
    tokens_here = expert_ids.shape[0]
    top_k = expert_ids.shape[1]
    slot_rows = experts_here * CAP
    all_slots = expert_groups * slot_rows
    flat_ids = expert_ids.reshape(-1)
    expert_hits = (
        flat_ids[:, None] == jnp.arange(expert_groups * experts_here, dtype=jnp.int32)[None, :]
    ).astype(jnp.int32)
    earlier = jnp.cumsum(expert_hits, axis=0) - expert_hits
    slot_index = jnp.sum(earlier * expert_hits, axis=1)
    target = flat_ids * CAP + slot_index
    placed = (target[:, None] == jnp.arange(all_slots, dtype=jnp.int32)[None, :]).reshape(
        tokens_here, top_k, all_slots
    )
    occupied = jnp.any(placed, axis=1).astype(jnp.bfloat16).reshape(
        tokens_here, expert_groups, experts_here, CAP
    )
    weights = (gate_scores / jnp.sum(gate_scores, axis=-1, keepdims=True)).astype(jnp.bfloat16)
    combine = jnp.sum(
        jnp.where(placed, weights[:, :, None].astype(jnp.float32), 0.0), axis=1
    ).astype(jnp.bfloat16).reshape(tokens_here, expert_groups, experts_here, CAP)
    normed_parts = normed.reshape(tokens_here, dp_groups, width_part)
    devices = expert_groups * dp_groups
    chunks = devices // dp_groups
    send_rows = jnp.einsum(
        "texc,tpw->xepcw", occupied, normed_parts, preferred_element_type=jnp.float32
    ).astype(jnp.bfloat16)
    mixed = jnp.zeros((tokens_here, dp_groups, width_part), jnp.float32)
    for x in range(experts_here):
        outgoing = send_rows[x].reshape(devices, CAP, width_part)
        grouped = lax.all_to_all(
            outgoing, ("expert", "dp"), split_axis=0, concat_axis=0, tiled=True
        )
        gate_part = jnp.einsum(
            "ncd,df->ncf", grouped, w_gate[x], preferred_element_type=jnp.float32
        )
        up_part = jnp.einsum("ncd,df->ncf", grouped, w_up[x], preferred_element_type=jnp.float32)
        parts = jnp.stack([gate_part, up_part], axis=1).astype(jnp.bfloat16)
        summed = lax.psum_scatter(parts, "dp", scatter_dimension=0, tiled=True)
        summed = summed.astype(jnp.float32)
        hidden_chunk = (jax.nn.silu(summed[:, 0]) * summed[:, 1]).astype(jnp.bfloat16)
        hidden = lax.all_gather(hidden_chunk, "dp", axis=0, tiled=True)
        expert_out = jnp.einsum(
            "ncf,fd->ncd", hidden, w_down[x], preferred_element_type=jnp.float32
        ).astype(jnp.bfloat16)
        returned = lax.all_to_all(
            expert_out, ("expert", "dp"), split_axis=0, concat_axis=0, tiled=True
        )
        back = returned.reshape(expert_groups, dp_groups, CAP, width_part)
        mixed = mixed + jnp.einsum(
            "tec,epcw->tpw", combine[:, :, x], back, preferred_element_type=jnp.float32
        )
    mixed_out = arrived_f + mixed.reshape(tokens_here, dp_groups * width_part)
    return mixed_out.astype(jnp.bfloat16)


def solution(mesh):
    in_specs = (
        P(("section", "expert", "dp"), None),
        P(),
        P(("section", "expert", "dp"), None),
        P(("section", "expert", "dp"), None),
        P("expert", "dp", None),
        P("expert", "dp", None),
        P("expert", None, "dp"),
    )
    out_specs = P(("section", "expert", "dp"), None)
    return jax.shard_map(
        per_device, mesh=mesh, in_specs=in_specs, out_specs=out_specs, check_vma=False
    )
```

```python
import jax
import jax.numpy as jnp
from jax import lax
from jax.sharding import PartitionSpec as P

CAP = 2


def passed_along(shard, axis, by):
    peers = lax.axis_size(axis)
    return lax.ppermute(shard, axis, [(i, (i + by) % peers) for i in range(peers)])


def per_device(panel, norm_gain, expert_ids, gate_scores, w_gate, w_up, w_down):
    arrived = passed_along(panel, "section", 1)
    arrived_f = arrived.astype(jnp.float32)
    mean_sq = jnp.mean(arrived_f * arrived_f, axis=-1, keepdims=True)
    normed = (arrived_f * lax.rsqrt(mean_sq + 1e-06) * norm_gain).astype(jnp.bfloat16)
    experts_here = w_gate.shape[0]
    width_part = w_gate.shape[1]
    expert_groups = lax.axis_size("expert")
    dp_groups = lax.axis_size("dp")
    tokens_here = expert_ids.shape[0]
    top_k = expert_ids.shape[1]
    slot_rows = experts_here * CAP
    all_slots = expert_groups * slot_rows
    flat_ids = expert_ids.reshape(-1)
    expert_hits = (
        flat_ids[:, None] == jnp.arange(expert_groups * experts_here, dtype=jnp.int32)[None, :]
    ).astype(jnp.int32)
    earlier = jnp.cumsum(expert_hits, axis=0) - expert_hits
    slot_index = jnp.sum(earlier * expert_hits, axis=1)
    target = flat_ids * CAP + slot_index
    placed = (target[:, None] == jnp.arange(all_slots, dtype=jnp.int32)[None, :]).reshape(
        tokens_here, top_k, all_slots
    )
    occupied = jnp.any(placed, axis=1).astype(jnp.bfloat16).reshape(
        tokens_here, expert_groups, slot_rows
    )
    normed_parts = normed.reshape(tokens_here, dp_groups, width_part)
    devices = expert_groups * dp_groups
    peer_rows = lax.all_to_all(normed_parts, "dp", split_axis=1, concat_axis=1, tiled=True)
    peer_occupied = lax.all_gather(occupied, "dp", axis=0, tiled=False)
    send_rows = jnp.einsum(
        "qtes,tqw->eqsw", peer_occupied, peer_rows, preferred_element_type=jnp.float32
    ).astype(jnp.bfloat16)
    incoming = lax.all_to_all(send_rows, "expert", split_axis=0, concat_axis=0, tiled=True)
    grouped = incoming.reshape(devices, experts_here, CAP, width_part)
    gate_part = jnp.einsum("nxcd,xdf->nxcf", grouped, w_gate, preferred_element_type=jnp.float32)
    up_part = jnp.einsum("nxcd,xdf->nxcf", grouped, w_up, preferred_element_type=jnp.float32)
    chunks = gate_part.shape[0] // dp_groups
    parts = jnp.stack(
        [
            gate_part.reshape(dp_groups, chunks, experts_here, CAP, -1),
            up_part.reshape(dp_groups, chunks, experts_here, CAP, -1),
        ],
        axis=1,
    ).astype(jnp.bfloat16)
    parts = lax.all_to_all(parts, "dp", split_axis=0, concat_axis=0, tiled=False)
    summed = jnp.sum(parts.astype(jnp.float32), axis=0)
    gate_full, up_full = summed[0], summed[1]
    hidden_chunk = (jax.nn.silu(gate_full) * up_full).astype(jnp.bfloat16)
    hidden = lax.all_gather(hidden_chunk, "dp", axis=0, tiled=True)
    hidden = hidden.reshape(devices, experts_here, CAP, -1)
    expert_out = jnp.einsum(
        "nxcf,xfd->nxcd", hidden, w_down, preferred_element_type=jnp.float32
    ).astype(jnp.bfloat16)
    returning = expert_out.reshape(devices, slot_rows, width_part)
    returned = lax.all_to_all(
        returning, ("expert", "dp"), split_axis=0, concat_axis=0, tiled=True
    )
    back = returned.reshape(expert_groups, dp_groups, slot_rows, width_part)
    weights = (gate_scores / jnp.sum(gate_scores, axis=-1, keepdims=True)).astype(jnp.bfloat16)
    combine = jnp.sum(
        jnp.where(placed, weights[:, :, None].astype(jnp.float32), 0.0), axis=1
    ).astype(jnp.bfloat16).reshape(tokens_here, expert_groups, slot_rows)
    mixed = jnp.einsum("tes,epsw->tpw", combine, back, preferred_element_type=jnp.float32)
    mixed_out = arrived_f + mixed.reshape(tokens_here, dp_groups * width_part)
    return mixed_out.astype(jnp.bfloat16)


def solution(mesh):
    in_specs = (
        P(("section", "expert", "dp"), None),
        P(),
        P(("section", "expert", "dp"), None),
        P(("section", "expert", "dp"), None),
        P("expert", "dp", None),
        P("expert", "dp", None),
        P("expert", None, "dp"),
    )
    out_specs = P(("section", "expert", "dp"), None)
    return jax.shard_map(
        per_device, mesh=mesh, in_specs=in_specs, out_specs=out_specs, check_vma=False
    )
```

```python
import jax
import jax.numpy as jnp
from jax import lax
from jax.sharding import PartitionSpec as P

CAP = 2


def passed_along(shard, axis, by):
    peers = lax.axis_size(axis)
    return lax.ppermute(shard, axis, [(i, (i + by) % peers) for i in range(peers)])


def per_device(panel, norm_gain, expert_ids, gate_scores, w_gate, w_up, w_down):
    arrived = passed_along(panel, "section", 1)
    arrived_f = arrived.astype(jnp.float32)
    mean_sq = jnp.mean(arrived_f * arrived_f, axis=-1, keepdims=True)
    normed = (arrived_f * lax.rsqrt(mean_sq + 1e-06) * norm_gain).astype(jnp.bfloat16)
    experts_here = w_gate.shape[0]
    width_part = w_gate.shape[1]
    expert_groups = lax.axis_size("expert")
    dp_groups = lax.axis_size("dp")
    tokens_here = expert_ids.shape[0]
    top_k = expert_ids.shape[1]
    slot_rows = experts_here * CAP
    all_slots = expert_groups * slot_rows
    flat_ids = expert_ids.reshape(-1)
    expert_hits = (
        flat_ids[:, None] == jnp.arange(expert_groups * experts_here, dtype=jnp.int32)[None, :]
    ).astype(jnp.int32)
    earlier = jnp.cumsum(expert_hits, axis=0) - expert_hits
    slot_index = jnp.sum(earlier * expert_hits, axis=1)
    target = flat_ids * CAP + slot_index
    placed = (target[:, None] == jnp.arange(all_slots, dtype=jnp.int32)[None, :]).reshape(
        tokens_here, top_k, all_slots
    )
    occupied = jnp.any(placed, axis=1).astype(jnp.bfloat16).reshape(
        tokens_here, expert_groups, slot_rows
    )
    normed_parts = normed.reshape(tokens_here, dp_groups, width_part)
    send_rows = jnp.einsum(
        "tes,tpw->epsw", occupied, normed_parts, preferred_element_type=jnp.float32
    ).astype(jnp.bfloat16)
    devices = expert_groups * dp_groups
    outgoing = send_rows.reshape(devices, slot_rows, width_part)
    incoming = lax.all_to_all(
        outgoing, ("expert", "dp"), split_axis=0, concat_axis=0, tiled=True
    )
    grouped = incoming.reshape(devices, experts_here, CAP, width_part)
    gate_part = jnp.einsum("nxcd,xdf->nxcf", grouped, w_gate, preferred_element_type=jnp.float32)
    up_part = jnp.einsum("nxcd,xdf->nxcf", grouped, w_up, preferred_element_type=jnp.float32)
    chunks = gate_part.shape[0] // dp_groups
    parts = jnp.stack(
        [
            gate_part.reshape(dp_groups, chunks, experts_here, CAP, -1),
            up_part.reshape(dp_groups, chunks, experts_here, CAP, -1),
        ],
        axis=1,
    ).astype(jnp.bfloat16)
    parts = lax.all_to_all(parts, "dp", split_axis=0, concat_axis=0, tiled=False)
    summed = jnp.sum(parts.astype(jnp.float32), axis=0)
    gate_full, up_full = summed[0], summed[1]
    hidden_chunk = (jax.nn.silu(gate_full) * up_full).astype(jnp.bfloat16)
    copies = jnp.broadcast_to(hidden_chunk[None], (dp_groups,) + hidden_chunk.shape)
    hidden = lax.all_to_all(copies, "dp", split_axis=0, concat_axis=0, tiled=False)
    hidden = hidden.reshape(devices, experts_here, CAP, -1)
    expert_out = jnp.einsum(
        "nxcf,xfd->nxcd", hidden, w_down, preferred_element_type=jnp.float32
    ).astype(jnp.bfloat16)
    returning = expert_out.reshape(devices, slot_rows, width_part)
    returned = lax.all_to_all(
        returning, ("expert", "dp"), split_axis=0, concat_axis=0, tiled=True
    )
    back = returned.reshape(expert_groups, dp_groups, slot_rows, width_part)
    weights = (gate_scores / jnp.sum(gate_scores, axis=-1, keepdims=True)).astype(jnp.bfloat16)
    combine = jnp.sum(
        jnp.where(placed, weights[:, :, None].astype(jnp.float32), 0.0), axis=1
    ).astype(jnp.bfloat16).reshape(tokens_here, expert_groups, slot_rows)
    mixed = jnp.einsum("tes,epsw->tpw", combine, back, preferred_element_type=jnp.float32)
    mixed_out = arrived_f + mixed.reshape(tokens_here, dp_groups * width_part)
    return mixed_out.astype(jnp.bfloat16)


def solution(mesh):
    in_specs = (
        P(("section", "expert", "dp"), None),
        P(),
        P(("section", "expert", "dp"), None),
        P(("section", "expert", "dp"), None),
        P("expert", "dp", None),
        P("expert", "dp", None),
        P("expert", None, "dp"),
    )
    out_specs = P(("section", "expert", "dp"), None)
    return jax.shard_map(
        per_device, mesh=mesh, in_specs=in_specs, out_specs=out_specs, check_vma=False
    )
```

```python
import jax
import jax.numpy as jnp
from jax import lax
from jax.sharding import PartitionSpec as P

CAP = 2


def passed_along(shard, axis, by):
    peers = lax.axis_size(axis)
    return lax.ppermute(shard, axis, [(i, (i + by) % peers) for i in range(peers)])


def per_device(panel, norm_gain, expert_ids, gate_scores, w_gate, w_up, w_down):
    panel_f = panel.astype(jnp.float32)
    mean_sq = jnp.mean(panel_f * panel_f, axis=-1, keepdims=True)
    normed_here = (panel_f * lax.rsqrt(mean_sq + 1e-06) * norm_gain).astype(jnp.bfloat16)
    arrived, normed = passed_along(jnp.stack([panel, normed_here]), "section", 1)
    arrived_f = arrived.astype(jnp.float32)
    experts_here = w_gate.shape[0]
    width_part = w_gate.shape[1]
    expert_groups = lax.axis_size("expert")
    dp_groups = lax.axis_size("dp")
    tokens_here = expert_ids.shape[0]
    top_k = expert_ids.shape[1]
    slot_rows = experts_here * CAP
    all_slots = expert_groups * slot_rows
    flat_ids = expert_ids.reshape(-1)
    expert_hits = (
        flat_ids[:, None] == jnp.arange(expert_groups * experts_here, dtype=jnp.int32)[None, :]
    ).astype(jnp.int32)
    earlier = jnp.cumsum(expert_hits, axis=0) - expert_hits
    slot_index = jnp.sum(earlier * expert_hits, axis=1)
    target = flat_ids * CAP + slot_index
    placed = (target[:, None] == jnp.arange(all_slots, dtype=jnp.int32)[None, :]).reshape(
        tokens_here, top_k, all_slots
    )
    occupied = jnp.any(placed, axis=1).astype(jnp.bfloat16).reshape(
        tokens_here, expert_groups, slot_rows
    )
    normed_parts = normed.reshape(tokens_here, dp_groups, width_part)
    send_rows = jnp.einsum(
        "tes,tpw->epsw", occupied, normed_parts, preferred_element_type=jnp.float32
    ).astype(jnp.bfloat16)
    devices = expert_groups * dp_groups
    outgoing = send_rows.reshape(devices, slot_rows, width_part)
    incoming = lax.all_to_all(
        outgoing, ("expert", "dp"), split_axis=0, concat_axis=0, tiled=True
    )
    grouped = incoming.reshape(devices, experts_here, CAP, width_part)
    gate_part = jnp.einsum("nxcd,xdf->nxcf", grouped, w_gate, preferred_element_type=jnp.float32)
    up_part = jnp.einsum("nxcd,xdf->nxcf", grouped, w_up, preferred_element_type=jnp.float32)
    chunks = gate_part.shape[0] // dp_groups
    parts = jnp.stack(
        [
            gate_part.reshape(dp_groups, chunks, experts_here, CAP, -1),
            up_part.reshape(dp_groups, chunks, experts_here, CAP, -1),
        ],
        axis=1,
    ).astype(jnp.bfloat16)
    parts = lax.all_to_all(parts, "dp", split_axis=0, concat_axis=0, tiled=False)
    summed = jnp.sum(parts.astype(jnp.float32), axis=0)
    gate_full, up_full = summed[0], summed[1]
    hidden_chunk = (jax.nn.silu(gate_full) * up_full).astype(jnp.bfloat16)
    hidden = lax.all_gather(hidden_chunk, "dp", axis=0, tiled=True)
    hidden = hidden.reshape(devices, experts_here, CAP, -1)
    expert_out = jnp.einsum(
        "nxcf,xfd->nxcd", hidden, w_down, preferred_element_type=jnp.float32
    ).astype(jnp.bfloat16)
    returning = expert_out.reshape(devices, slot_rows, width_part)
    returned = lax.all_to_all(
        returning, ("expert", "dp"), split_axis=0, concat_axis=0, tiled=True
    )
    back = returned.reshape(expert_groups, dp_groups, slot_rows, width_part)
    weights = (gate_scores / jnp.sum(gate_scores, axis=-1, keepdims=True)).astype(jnp.bfloat16)
    combine = jnp.sum(
        jnp.where(placed, weights[:, :, None].astype(jnp.float32), 0.0), axis=1
    ).astype(jnp.bfloat16).reshape(tokens_here, expert_groups, slot_rows)
    mixed = jnp.einsum("tes,epsw->tpw", combine, back, preferred_element_type=jnp.float32)
    mixed_out = arrived_f + mixed.reshape(tokens_here, dp_groups * width_part)
    return mixed_out.astype(jnp.bfloat16)


def solution(mesh):
    in_specs = (
        P(("section", "expert", "dp"), None),
        P(),
        P(("section", "expert", "dp"), None),
        P(("section", "expert", "dp"), None),
        P("expert", "dp", None),
        P("expert", "dp", None),
        P("expert", None, "dp"),
    )
    out_specs = P(("section", "expert", "dp"), None)
    return jax.shard_map(
        per_device, mesh=mesh, in_specs=in_specs, out_specs=out_specs, check_vma=False
    )
```

```python
import jax
import jax.numpy as jnp
from jax import lax
from jax.sharding import PartitionSpec as P

CAP = 2


def passed_along(shard, axis, by):
    peers = lax.axis_size(axis)
    return lax.ppermute(shard, axis, [(i, (i + by) % peers) for i in range(peers)])


def per_device(panel, norm_gain, expert_ids, gate_scores, w_gate, w_up, w_down):
    arrived = passed_along(panel, "section", 1)
    arrived_f = arrived.astype(jnp.float32)
    mean_sq = jnp.mean(arrived_f * arrived_f, axis=-1, keepdims=True)
    normed = (arrived_f * lax.rsqrt(mean_sq + 1e-06) * norm_gain).astype(jnp.bfloat16)
    experts_here = w_gate.shape[0]
    width_part = w_gate.shape[1]
    expert_groups = lax.axis_size("expert")
    dp_groups = lax.axis_size("dp")
    tokens_here = expert_ids.shape[0]
    top_k = expert_ids.shape[1]
    slot_rows = experts_here * CAP
    all_slots = expert_groups * slot_rows
    flat_ids = expert_ids.reshape(-1)
    expert_hits = (
        flat_ids[:, None] == jnp.arange(expert_groups * experts_here, dtype=jnp.int32)[None, :]
    ).astype(jnp.int32)
    earlier = jnp.cumsum(expert_hits, axis=0) - expert_hits
    slot_index = jnp.sum(earlier * expert_hits, axis=1)
    target = flat_ids * CAP + slot_index
    placed = (target[:, None] == jnp.arange(all_slots, dtype=jnp.int32)[None, :]).reshape(
        tokens_here, top_k, all_slots
    )
    occupied = jnp.any(placed, axis=1).astype(jnp.bfloat16).reshape(
        tokens_here, expert_groups, slot_rows
    )
    normed_parts = normed.reshape(tokens_here, dp_groups, width_part)
    send_rows = jnp.einsum(
        "tes,tpw->epsw", occupied, normed_parts, preferred_element_type=jnp.float32
    ).astype(jnp.bfloat16)
    devices = expert_groups * dp_groups
    outgoing = send_rows.reshape(devices, slot_rows, width_part)
    incoming = lax.all_to_all(
        outgoing, ("expert", "dp"), split_axis=0, concat_axis=0, tiled=True
    )
    grouped = incoming.reshape(devices, experts_here, CAP, width_part)
    gate_part = jnp.einsum("nxcd,xdf->nxcf", grouped, w_gate, preferred_element_type=jnp.float32)
    up_part = jnp.einsum("nxcd,xdf->nxcf", grouped, w_up, preferred_element_type=jnp.float32)
    chunks = gate_part.shape[0] // dp_groups
    gate_full, up_full = (
        jnp.sum(
            lax.all_to_all(
                part.reshape(dp_groups, chunks, experts_here, CAP, -1).astype(jnp.bfloat16),
                "dp",
                split_axis=0,
                concat_axis=0,
                tiled=False,
            ).astype(jnp.float32),
            axis=0,
        )
        for part in (gate_part, up_part)
    )
    hidden_chunk = (jax.nn.silu(gate_full) * up_full).astype(jnp.bfloat16)
    hidden = lax.all_gather(hidden_chunk, "dp", axis=0, tiled=True)
    hidden = hidden.reshape(devices, experts_here, CAP, -1)
    expert_out = jnp.einsum(
        "nxcf,xfd->nxcd", hidden, w_down, preferred_element_type=jnp.float32
    ).astype(jnp.bfloat16)
    returning = expert_out.reshape(devices, slot_rows, width_part)
    returned = lax.all_to_all(
        returning, ("expert", "dp"), split_axis=0, concat_axis=0, tiled=True
    )
    back = returned.reshape(expert_groups, dp_groups, slot_rows, width_part)
    weights = (gate_scores / jnp.sum(gate_scores, axis=-1, keepdims=True)).astype(jnp.bfloat16)
    combine = jnp.sum(
        jnp.where(placed, weights[:, :, None].astype(jnp.float32), 0.0), axis=1
    ).astype(jnp.bfloat16).reshape(tokens_here, expert_groups, slot_rows)
    mixed = jnp.einsum("tes,epsw->tpw", combine, back, preferred_element_type=jnp.float32)
    mixed_out = arrived_f + mixed.reshape(tokens_here, dp_groups * width_part)
    return mixed_out.astype(jnp.bfloat16)


def solution(mesh):
    in_specs = (
        P(("section", "expert", "dp"), None),
        P(),
        P(("section", "expert", "dp"), None),
        P(("section", "expert", "dp"), None),
        P("expert", "dp", None),
        P("expert", "dp", None),
        P("expert", None, "dp"),
    )
    out_specs = P(("section", "expert", "dp"), None)
    return jax.shard_map(
        per_device, mesh=mesh, in_specs=in_specs, out_specs=out_specs, check_vma=False
    )
```
